128 devices in a mesh: tm: 16 (over x, z_lo, core), agent: 8 (over y, z_hi).
Axes of the slice: x: 4, y: 4, z: 4 (z_hi: 2, z_lo: 2; z = z_hi * 2 + z_lo), core: 2. Of those that a mesh axis runs over, the one named last changes fastest.
Arguments:
- states: bfloat16 [96, 1024, 512], P('tm', 'agent'), may hold values from -30 to 30
- neighbours: int32 [8, 4], replicated, may hold values from 0 to 7, as said below
- w_query_t: bfloat16 [512, 512], replicated, may hold values from -16 to 16
- w_key_t: bfloat16 [512, 512], replicated, may hold values from -16 to 16
- w_value_t: bfloat16 [512, 512], replicated, may hold values from -0.25 to 0.25
- w_out_t: bfloat16 [512, 512], replicated, may hold values from -0.25 to 0.25
- w_query_a: bfloat16 [512, 512], replicated, may hold values from -16 to 16
- w_key_a: bfloat16 [512, 512], replicated, may hold values from -16 to 16
- w_value_a: bfloat16 [512, 512], replicated, may hold values from -0.25 to 0.25
- w_out_a: bfloat16 [512, 512], replicated, may hold values from -0.25 to 0.25
- w_in: bfloat16 [512, 2048], replicated, may hold values from -0.25 to 0.25
- w_mlp_out: bfloat16 [2048, 512], replicated, may hold values from -0.125 to 0.125
Outputs:
- mixed: bfloat16 [96, 1024, 512], P('tm', 'agent')
The draws below stay inside these ranges and needn't reach their ends.
Inputs may be any that keep to these rules, and one draw needn't show every extreme that they name: neighbours[b] lists 4 different blocks, the first of them b itself.
All inputs are finite; a program needn't handle non-finite values.
Results may differ from the reference program's by a relative error of at most 0.006.
Values may be sent and summed in bfloat16 or wider, within the bound.
A program may use at most 128 MiB of HBM per device.

```python
import math
import jax
import jax.numpy as jnp
from jax import lax

D = 512
HEADS = 8
FF = 2048
BLK = 128
NEIGH = 4
TIME = 96
NBLK = 8
AGENTS = 1024


def draw_states(key, part):
    fold = jax.random.fold_in
    base = jax.random.normal(fold(key, 1), (TIME, AGENTS, D), jnp.float32)
    row_scale = jnp.exp(jax.random.uniform(fold(key, 2), (TIME, AGENTS, 1), jnp.float32) * math.log(10.0))
    col_scale = jnp.exp(jax.random.uniform(fold(key, 3), (1, 1, D), jnp.float32) * math.log(10.0))
    return jnp.clip(base * row_scale * col_scale / 10.0, -30.0, 30.0).astype(jnp.bfloat16)


def paired_weights(key, salt):
    fold = jax.random.fold_in
    query_w = jax.random.normal(fold(key, salt), (D, D), jnp.float32) * D ** (-0.5)
    key_w = jax.random.normal(fold(key, salt + 1), (D, D), jnp.float32) * D ** (-0.5)
    return (query_w, key_w)


def draw_w_query_t(key, part):
    return paired_weights(key, 10)[0].astype(jnp.bfloat16)


def draw_w_key_t(key, part):
    return paired_weights(key, 10)[1].astype(jnp.bfloat16)


def draw_w_query_a(key, part):
    return paired_weights(key, 20)[0].astype(jnp.bfloat16)


def draw_w_key_a(key, part):
    return paired_weights(key, 20)[1].astype(jnp.bfloat16)


def draw_neighbours(key, part):
    row_keys = jax.random.split(jax.random.fold_in(key, 30), NBLK)

    def one_row(row_key, block):
        order = jax.random.permutation(row_key, NBLK - 1)[:NEIGH - 1].astype(jnp.int32)
        others = order + (order >= block).astype(jnp.int32)
        return jnp.concatenate([block[None], others])
    return jax.vmap(one_row)(row_keys, jnp.arange(NBLK, dtype=jnp.int32))


def centred(own_key, extent, deviation, limit, kind=jnp.bfloat16):
    entries = jax.random.normal(own_key, extent, jnp.float32) * deviation
    return jnp.minimum(jnp.maximum(entries, -limit), limit).astype(kind)


def setup_inputs(seed: int = 0) -> dict:
    streams_of = jax.random.split(jax.random.key(seed), 13)
    states = draw_states(jax.random.fold_in(streams_of[12], 71), 0)
    neighbours = draw_neighbours(jax.random.fold_in(streams_of[12], 71), 0)
    w_query_t = draw_w_query_t(jax.random.fold_in(streams_of[12], 71), 0)
    w_key_t = draw_w_key_t(jax.random.fold_in(streams_of[12], 71), 0)
    w_value_t = centred(streams_of[4], (D, D), D ** -0.5, 0.25)
    w_out_t = centred(streams_of[5], (D, D), D ** -0.5, 0.25)
    w_query_a = draw_w_query_a(jax.random.fold_in(streams_of[12], 71), 0)
    w_key_a = draw_w_key_a(jax.random.fold_in(streams_of[12], 71), 0)
    w_value_a = centred(streams_of[8], (D, D), D ** -0.5, 0.25)
    w_out_a = centred(streams_of[9], (D, D), D ** -0.5, 0.25)
    w_in = centred(streams_of[10], (D, FF), D ** -0.5, 0.25)
    w_mlp_out = centred(streams_of[11], (FF, D), FF ** -0.5, 0.125)
    return {"states": states, "neighbours": neighbours, "w_query_t": w_query_t, "w_key_t": w_key_t, "w_value_t": w_value_t, "w_out_t": w_out_t, "w_query_a": w_query_a, "w_key_a": w_key_a, "w_value_a": w_value_a, "w_out_a": w_out_a, "w_in": w_in, "w_mlp_out": w_mlp_out}


negative_floor = -1e+30
epsilon = 1e-06

def rms_normed(values):
    wide = values.astype(jnp.float32)
    scale = lax.rsqrt(lax.optimization_barrier(jnp.mean(wide * wide, axis=-1, keepdims=True)) + epsilon)
    return (wide * scale).astype(jnp.bfloat16)

def project(normed, weight):
    return jnp.dot(normed, weight, preferred_element_type=jnp.float32).astype(jnp.bfloat16)

def attend(query, keys, values, allowed):
    batch, query_len, features = query.shape
    key_len = keys.shape[1]
    head_size = features // HEADS
    query_h = query.reshape(batch, query_len, HEADS, head_size).astype(jnp.float32)
    keys_h = keys.reshape(batch, key_len, HEADS, head_size).astype(jnp.float32)
    values_h = values.reshape(batch, key_len, HEADS, head_size).astype(jnp.float32)
    scores = jnp.einsum('bqhe,bkhe->bhqk', query_h, keys_h) * head_size ** (-0.5)
    scores = jnp.where(allowed[:, None], scores, negative_floor)
    largest = lax.optimization_barrier(jnp.max(scores, axis=-1, keepdims=True))
    weights = jnp.where(allowed[:, None], jnp.exp(scores - largest), 0.0)
    totals = lax.optimization_barrier(jnp.sum(weights, axis=-1))
    rounded = lax.optimization_barrier(weights.astype(jnp.bfloat16)).astype(jnp.float32)
    summed = jnp.einsum('bhqk,bkhe->bqhe', rounded, values_h)
    result = summed / jnp.transpose(totals, (0, 2, 1))[..., None]
    return result.reshape(batch, query_len, features).astype(jnp.bfloat16)

def reference(states, neighbours, w_query_t, w_key_t, w_value_t, w_out_t, w_query_a, w_key_a, w_value_a, w_out_a, w_in, w_mlp_out):

    def time_block(block_states):
        normed = rms_normed(block_states)
        query = jnp.swapaxes(project(normed, w_query_t), 0, 1)
        keys = jnp.swapaxes(project(normed, w_key_t), 0, 1)
        values = jnp.swapaxes(project(normed, w_value_t), 0, 1)
        steps = jnp.arange(TIME)
        allowed = (steps[None, :] <= steps[:, None])[None]
        mixed_time = jnp.swapaxes(attend(query, keys, values, allowed), 0, 1)
        added = block_states.astype(jnp.float32) + jnp.dot(mixed_time, w_out_t, preferred_element_type=jnp.float32)
        return added.astype(jnp.bfloat16)
    blocks = jnp.transpose(states.reshape(TIME, NBLK, BLK, D), (1, 0, 2, 3))
    after_time = jnp.transpose(lax.map(time_block, blocks), (1, 0, 2, 3)).reshape(TIME, AGENTS, D)

    def agent_step(row_states):
        normed = rms_normed(row_states)
        query = project(normed, w_query_a).reshape(NBLK, BLK, D)
        keys = project(normed, w_key_a).reshape(NBLK, BLK, D)[neighbours].reshape(NBLK, NEIGH * BLK, D)
        values = project(normed, w_value_a).reshape(NBLK, BLK, D)[neighbours].reshape(NBLK, NEIGH * BLK, D)
        allowed = jnp.ones((1, BLK, NEIGH * BLK), dtype=bool)
        mixed_agent = attend(query, keys, values, allowed).reshape(AGENTS, D)
        after_agent = (row_states.astype(jnp.float32) + jnp.dot(mixed_agent, w_out_a, preferred_element_type=jnp.float32)).astype(jnp.bfloat16)
        inner = jax.nn.gelu(jnp.dot(rms_normed(after_agent), w_in, preferred_element_type=jnp.float32), approximate=True).astype(jnp.bfloat16)
        final = after_agent.astype(jnp.float32) + jnp.dot(inner, w_mlp_out, preferred_element_type=jnp.float32)
        return final.astype(jnp.bfloat16)
    return lax.map(agent_step, after_time)
```

```python
import functools

import jax
import jax.numpy as jnp
from jax import lax
from jax.experimental import pallas as pl
from jax.experimental.pallas import tpu as pltpu
from jax.sharding import PartitionSpec as P

MESH = pl.DeviceIdType.MESH
HEADS = 8
epsilon = 1e-06
negative_floor = -1e30
bf16 = jnp.bfloat16
f32 = jnp.float32


def normed(wide):
    return (wide * lax.rsqrt(jnp.mean(wide * wide, axis=-1, keepdims=True) + epsilon)).astype(bf16)


def mm(a, b):
    return jnp.dot(a, b, preferred_element_type=f32)


def mm_nt(a, b):
    return lax.dot_general(a, b, (((1,), (1,)), ((), ())), preferred_element_type=f32)


def two_heads(query):
    low = lax.broadcasted_iota(jnp.int32, query.shape, 1) < 64
    none = jnp.zeros_like(query)
    return jnp.concatenate([jnp.where(low, query, none), jnp.where(low, none, query)], axis=0)


def join_heads(stacked):
    n = stacked.shape[0] // 2
    low = lax.broadcasted_iota(jnp.int32, (n, 128), 1) < 64
    return jnp.where(low, stacked[:n], stacked[n:])


def kernel(
    groups, blocks, steps, agents, near,
    states_hbm, nb_ref, wqt_hbm, wkt_hbm, wvt_hbm, wot_hbm, wqa_hbm, wka_hbm, wva_hbm, woa_hbm, win_hbm, wmo_hbm,
    out_hbm,
    states, wide, wqt, wkt, wvt, wot, wqa, wka, wva, woa, win, wmo,
    send1, recv1, qf, kf, vf, mask, mixed_t, send2, recv2, after, aft_b, qkv, ret, am, outs,
    in_sem, out_sem, s1, r1, s2, r2, s3, r3, s4, r4, self3, self4, *recv3,
):
    tm = lax.axis_index("tm")
    ag = lax.axis_index("agent")
    sub = agents // groups
    rows = steps * sub
    half_steps = steps // 2
    pairs = HEADS // 2

    def tm_peer(k):
        return lax.rem(tm + k + groups, groups)

    def ag_peer(k):
        return lax.rem(ag + k + blocks, blocks)

    loads = [
        pltpu.make_async_copy(source, target, in_sem.at[n])
        for n, (source, target) in enumerate(
            [(states_hbm, states), (wqt_hbm, wqt), (wkt_hbm, wkt), (wvt_hbm, wvt), (wot_hbm, wot), (wqa_hbm, wqa),
             (wka_hbm, wka), (wva_hbm, wva), (woa_hbm, woa), (win_hbm, win), (wmo_hbm, wmo)]
        )
    ]
    for load in loads:
        load.start()
    barrier = pltpu.get_barrier_semaphore()
    for k in range(1, groups):
        pl.semaphore_signal(barrier, inc=1, device_id={"tm": tm_peer(k)}, device_id_type=MESH)
    for k in range(1, blocks):
        pl.semaphore_signal(barrier, inc=1, device_id={"agent": ag_peer(k)}, device_id_type=MESH)

    loads[0].wait()
    wide[...] = states[...].astype(f32)
    pl.semaphore_wait(barrier, groups + blocks - 2)

    first = []
    for k in list(range(1, groups)) + [0]:
        base = pl.multiple_of(tm_peer(k) * sub, sub)
        piece = jnp.concatenate([wide[t, pl.ds(base, sub), :] for t in range(steps)], axis=0).astype(bf16)
        if k == 0:
            recv1[0] = piece
            continue
        send1[k] = piece
        copy = pltpu.make_async_remote_copy(
            src_ref=send1.at[k], dst_ref=recv1.at[k], send_sem=s1.at[k], recv_sem=r1.at[k],
            device_id={"tm": tm_peer(k)}, device_id_type=MESH,
        )
        copy.start()
        first.append(copy)

    total_steps = groups * steps

    def times(shape, axis):
        row = lax.broadcasted_iota(jnp.int32, shape, axis).astype(f32)
        row = jnp.where(row >= total_steps, row - total_steps, row)
        slot = jnp.floor((row + 0.5) / steps)
        owner = tm.astype(f32) - slot
        owner = jnp.where(owner < 0, owner + groups, owner)
        return row + steps * (owner - slot)

    shape = (2 * total_steps, total_steps)
    mask[...] = jnp.where(times(shape, 1) <= times(shape, 0), 0.0, negative_floor)

    for load in loads[1:4]:
        load.wait()
    batch = 4
    for g in range(groups // batch):
        for k in range(g * batch, (g + 1) * batch):
            if k:
                first[k - 1].wait_recv()
        there = pl.ds(g * batch * rows, batch * rows)
        flat = normed(recv1[g * batch:(g + 1) * batch].reshape(batch * rows, 512).astype(f32))
        for target, weight, scale in ((qf, wqt, 0.125), (kf, wkt, None), (vf, wvt, None)):
            result = mm(flat, weight[...])
            if scale is not None:
                result = result * scale
            for h in range(pairs):
                target[h, there, :] = result[:, h * 128:(h + 1) * 128]

    def one_agent(a, carry):
        mine = pl.ds(a, total_steps, stride=sub)
        for h in range(pairs):
            query = two_heads(qf[h, mine, :].astype(bf16))
            scores = mm_nt(query, kf[h, mine, :].astype(bf16)) + mask[...]
            weights = jnp.exp(scores - jnp.max(scores, axis=-1, keepdims=True))
            totals = jnp.sum(weights, axis=-1, keepdims=True)
            summed = mm(weights.astype(bf16), vf[h, mine, :].astype(bf16))
            mixed_t[h, mine, :] = join_heads(summed / totals)
        return carry

    lax.fori_loop(0, sub, one_agent, 0)

    second = []
    for k in list(range(1, groups)) + [0]:
        piece = jnp.concatenate([mixed_t[h, pl.ds(k * rows, rows), :] for h in range(pairs)], axis=1).astype(bf16)
        if k == 0:
            recv2[0] = piece
            continue
        send2[k] = piece
        copy = pltpu.make_async_remote_copy(
            src_ref=send2.at[k], dst_ref=recv2.at[k], send_sem=s2.at[k], recv_sem=r2.at[k],
            device_id={"tm": tm_peer(-k)}, device_id_type=MESH,
        )
        copy.start()
        second.append(copy)

    loads[4].wait()
    for g in range(groups // batch):
        for k in range(g * batch, (g + 1) * batch):
            if k:
                second[k - 1].wait_recv()
        added = mm(recv2[g * batch:(g + 1) * batch].reshape(batch * rows, 512), wot[...])
        for k in range(batch):
            base = pl.multiple_of(tm_peer(g * batch + k) * sub, sub)
            for t in range(steps):
                after[t, pl.ds(base, sub), :] = added[(k * steps + t) * sub:(k * steps + t + 1) * sub]

    for load in loads[5:8]:
        load.wait()
    my_half = ag // pairs
    my_pair = lax.rem(ag, pairs)
    my_lanes = pl.ds(pl.multiple_of(my_pair * 128, 128), 128)
    third = []
    for t in range(half_steps):
        both = [
            (wide[t + h * half_steps] + after[t + h * half_steps]).astype(bf16) for h in range(2)
        ]
        for h in range(2):
            aft_b[t + h * half_steps] = both[h]
        flat = normed(jnp.concatenate(both, axis=0).astype(f32))
        for n, (weight, scale) in enumerate([(wqa, 0.125), (wka, 1.0), (wva, 1.0)]):
            result = mm(flat, weight[...])
            if n == 0:
                result = result * scale
            result = result.astype(bf16)
            for h in range(2):
                qkv[t, h, n] = result[h * agents:(h + 1) * agents]
        for k in range(1, blocks):
            peer = ag_peer(k)
            lanes = pl.ds(pl.multiple_of(lax.rem(peer, pairs) * 128, 128), 128)
            copy = pltpu.make_async_remote_copy(
                src_ref=qkv.at[t, peer // pairs, :, :, lanes], dst_ref=recv3[t].at[k],
                send_sem=s3.at[t, k], recv_sem=r3.at[t, k],
                device_id={"agent": peer}, device_id_type=MESH,
            )
            copy.start()
            third.append(copy)
        own = pltpu.make_async_copy(qkv.at[t, my_half, :, :, my_lanes], recv3[t].at[0], self3.at[t])
        own.start()
        third.append(own)

    fourth = []

    def attention(t):
        for copy in third[t * blocks:(t + 1) * blocks - 1]:
            copy.wait_recv()
        third[(t + 1) * blocks - 1].wait()

        def one_block(k, carry):
            block = ag_peer(-k)
            query = two_heads(recv3[t][k, 0])
            slots = [lax.rem(ag - nb_ref[block, j] + blocks, blocks) for j in range(near)]
            keys = jnp.concatenate([recv3[t][slot, 1] for slot in slots], axis=0)
            values = jnp.concatenate([recv3[t][slot, 2] for slot in slots], axis=0)
            scores = mm_nt(query, keys)
            weights = jnp.exp(scores - jnp.max(scores, axis=-1, keepdims=True))
            totals = jnp.sum(weights, axis=-1, keepdims=True)
            summed = mm(weights.astype(bf16), values)
            ret[t, k] = join_heads(summed / totals).astype(bf16)
            return carry

        lax.fori_loop(0, blocks, one_block, 0)
        target = am.at[my_half * half_steps + t, :, my_lanes]
        for k in range(1, blocks):
            copy = pltpu.make_async_remote_copy(
                src_ref=ret.at[t, k], dst_ref=target, send_sem=s4.at[t, k], recv_sem=r4.at[t, k],
                device_id={"agent": ag_peer(-k)}, device_id_type=MESH,
            )
            copy.start()
            fourth.append(copy)
        own = pltpu.make_async_copy(ret.at[t, 0], target, self4.at[t])
        own.start()
        fourth.append(own)

    stores = []

    def tail(t):
        for copy in fourth[t * blocks:(t + 1) * blocks - 1]:
            copy.wait_recv()
        fourth[(t + 1) * blocks - 1].wait()
        where = [t, t + half_steps]
        both = jnp.concatenate([am[w] for w in where], axis=0)
        base = jnp.concatenate([aft_b[w] for w in where], axis=0).astype(f32)
        after_agent = (base + mm(both, woa[...])).astype(bf16).astype(f32)
        inner = jax.nn.gelu(mm(normed(after_agent), win[...]), approximate=True).astype(bf16)
        final = (after_agent + mm(inner, wmo[...])).astype(bf16)
        for n, w in enumerate(where):
            outs[w] = final[n * agents:(n + 1) * agents]
            store = pltpu.make_async_copy(outs.at[w], out_hbm.at[w], out_sem.at[w])
            store.start()
            stores.append(store)

    attention(0)
    for load in loads[8:]:
        load.wait()
    for t in range(1, half_steps):
        attention(t)
        tail(t - 1)
    tail(half_steps - 1)

    for copy in first + second:
        copy.wait_send()
    for t in range(half_steps):
        for copy in third[t * blocks:(t + 1) * blocks - 1] + fourth[t * blocks:(t + 1) * blocks - 1]:
            copy.wait_send()
    for store in stores:
        store.wait()


def local(
    groups, blocks,
    states, neighbours, w_query_t, w_key_t, w_value_t, w_out_t, w_query_a, w_key_a, w_value_a, w_out_a, w_in, w_mlp_out,
):
    steps, agents, width = states.shape
    hidden = w_in.shape[1]
    rows = steps * (agents // groups)
    total = groups * steps
    square = (width, width)
    half = steps // 2
    anywhere = pl.BlockSpec(memory_space=pl.ANY)
    dma = pltpu.SemaphoreType.DMA
    return pl.pallas_call(
        functools.partial(kernel, groups, blocks, steps, agents, neighbours.shape[1]),
        out_shape=jax.ShapeDtypeStruct(states.shape, bf16),
        in_specs=[anywhere, pl.BlockSpec(memory_space=pltpu.SMEM)] + [anywhere] * 10,
        out_specs=anywhere,
        scratch_shapes=[
            pltpu.VMEM(states.shape, bf16),
            pltpu.VMEM(states.shape, f32),
            *[pltpu.VMEM(square, bf16)] * 8,
            pltpu.VMEM((width, hidden), bf16),
            pltpu.VMEM((hidden, width), bf16),
            pltpu.VMEM((groups, rows, width), bf16),
            pltpu.VMEM((groups, rows, width), bf16),
            *[pltpu.VMEM((width // 128, groups * rows, 128), f32)] * 3,
            pltpu.VMEM((2 * total, total), f32),
            pltpu.VMEM((width // 128, groups * rows, 128), f32),
            pltpu.VMEM((groups, rows, width), bf16),
            pltpu.VMEM((groups, rows, width), bf16),
            pltpu.VMEM(states.shape, f32),
            pltpu.VMEM(states.shape, bf16),
            pltpu.VMEM((half, 2, 3, agents, width), bf16),
            pltpu.VMEM((half, blocks, agents, 128), bf16),
            pltpu.VMEM(states.shape, bf16),
            pltpu.VMEM(states.shape, bf16),
            dma((11,)), dma((steps,)),
            dma((groups,)), dma((groups,)), dma((groups,)), dma((groups,)),
            dma((half, blocks)), dma((half, blocks)), dma((half, blocks)), dma((half, blocks)),
            dma((half,)), dma((half,)),
            *[pltpu.VMEM((blocks, 3, agents, 128), bf16)] * half,
        ],
        compiler_params=pltpu.CompilerParams(
            collective_id=0, has_side_effects=True, vmem_limit_bytes=60 * 1024 * 1024
        ),
    )(states, neighbours, w_query_t, w_key_t, w_value_t, w_out_t, w_query_a, w_key_a, w_value_a, w_out_a, w_in, w_mlp_out)


def solution(mesh):
    placed = (P("tm", "agent", None), P(), P(), P(), P(), P(), P(), P(), P(), P(), P(), P())
    return jax.shard_map(
        functools.partial(local, mesh.shape["tm"], mesh.shape["agent"]),
        mesh=mesh, in_specs=placed, out_specs=P("tm", "agent", None), check_vma=False,
    )
```

```python
import functools

import jax
import jax.numpy as jnp
from jax import lax
from jax.experimental import pallas as pl
from jax.experimental.pallas import tpu as pltpu
from jax.sharding import PartitionSpec as P

MESH = pl.DeviceIdType.MESH
HEADS = 8
epsilon = 1e-06
negative_floor = -1e30
bf16 = jnp.bfloat16
f32 = jnp.float32


def normed(wide):
    return (wide * lax.rsqrt(jnp.mean(wide * wide, axis=-1, keepdims=True) + epsilon)).astype(bf16)


def mm(a, b):
    return jnp.dot(a, b, preferred_element_type=f32)


def mm_nt(a, b):
    return lax.dot_general(a, b, (((1,), (1,)), ((), ())), preferred_element_type=f32)


def two_heads(query):
    low = lax.broadcasted_iota(jnp.int32, query.shape, 1) < 64
    none = jnp.zeros_like(query)
    return jnp.concatenate([jnp.where(low, query, none), jnp.where(low, none, query)], axis=0)


def join_heads(stacked):
    n = stacked.shape[0] // 2
    low = lax.broadcasted_iota(jnp.int32, (n, 128), 1) < 64
    return jnp.where(low, stacked[:n], stacked[n:])


def kernel(
    groups, blocks, steps, agents, near,
    states_hbm, nb_hbm, wqt_hbm, wkt_hbm, wvt_hbm, wot_hbm, wqa_hbm, wka_hbm, wva_hbm, woa_hbm, win_hbm, wmo_hbm,
    out_hbm,
    nb_ref, states, wide, wqt, wkt, wvt, wot, wqa, wka, wva, wqb, wkb, wvb, woa, win, wmo,
    send1, recv1, qf, kf, vf, mask, mixed_t, send2, recv2, after, aft_b, tokens, all_full, all_part,
    qkv_full, qkv_part, ret_full, ret_part, am, outs,
    in_sem, out_sem, s1, r1, s2, r2, s3, r3, s4, r4, s5, r5,
):
    tm = lax.axis_index("tm")
    ag = lax.axis_index("agent")
    core = lax.rem(tm, 2)
    sub = agents // groups
    rows = steps * sub
    pairs = HEADS // 2
    half = agents // 2

    def tm_peer(k):
        return lax.rem(tm + k + groups, groups)

    def ag_peer(k):
        return lax.rem(ag + k + blocks, blocks)

    duo, side = ag // 2, lax.rem(ag, 2)
    full_core, full_step = side, duo
    part_core, part_step = duo // 2, 4 + lax.rem(duo, 2)
    full_lanes = pl.ds(pl.multiple_of(core * 256, 256), 256)
    part_lanes = pl.ds(pl.multiple_of((side * 2 + core) * 128, 128), 128)

    sources = [(states_hbm, states), (nb_hbm, nb_ref), (wqt_hbm, wqt), (wkt_hbm, wkt), (wvt_hbm, wvt), (wot_hbm, wot)]
    for hbm, wide_cols, few_cols in ((wqa_hbm, wqa, wqb), (wka_hbm, wka, wkb), (wva_hbm, wva, wvb)):
        sources += [(hbm.at[:, full_lanes], wide_cols), (hbm.at[:, part_lanes], few_cols)]
    sources += [(woa_hbm, woa), (win_hbm, win), (wmo_hbm, wmo)]
    loads = [pltpu.make_async_copy(source, target, in_sem.at[n]) for n, (source, target) in enumerate(sources)]
    loads[0].start()
    barrier = pltpu.get_barrier_semaphore()
    for k in range(1, groups):
        pl.semaphore_signal(barrier, inc=1, device_id={"tm": tm_peer(k)}, device_id_type=MESH)
    for k in range(1, blocks):
        for c in range(2):
            pl.semaphore_signal(
                barrier, inc=1, device_id={"tm": tm - core + c, "agent": ag_peer(k)}, device_id_type=MESH
            )
    for load in loads[1:]:
        load.start()

    loads[0].wait()
    wide[...] = states[...].astype(f32)
    for k in range(groups):
        base = pl.multiple_of(tm_peer(k) * sub, sub)
        piece = jnp.concatenate([wide[t, pl.ds(base, sub), :] for t in range(steps)], axis=0).astype(bf16)
        if k == 0:
            recv1[0] = piece
        else:
            send1[k] = piece
    pl.semaphore_wait(barrier, groups - 1 + 2 * (blocks - 1))
    first = []
    for k in range(1, groups):
        copy = pltpu.make_async_remote_copy(
            src_ref=send1.at[k], dst_ref=recv1.at[k], send_sem=s1.at[k], recv_sem=r1.at[k],
            device_id={"tm": tm_peer(k)}, device_id_type=MESH,
        )
        copy.start()
        first.append(copy)

    total_steps = groups * steps

    def times(shape, axis):
        row = lax.broadcasted_iota(jnp.int32, shape, axis).astype(f32)
        row = jnp.where(row >= total_steps, row - total_steps, row)
        slot = jnp.floor((row + 0.5) / steps)
        owner = tm.astype(f32) - slot
        owner = jnp.where(owner < 0, owner + groups, owner)
        return row + steps * (owner - slot)

    shape = (2 * total_steps, total_steps)
    mask[...] = jnp.where(times(shape, 1) <= times(shape, 0), 0.0, negative_floor)

    for load in loads[1:5]:
        load.wait()
    batch = 4
    for g in range(groups // batch):
        for k in range(g * batch, (g + 1) * batch):
            if k:
                first[k - 1].wait_recv()
        there = pl.ds(g * batch * rows, batch * rows)
        flat = normed(recv1[g * batch:(g + 1) * batch].reshape(batch * rows, 512).astype(f32))
        for target, weight, scale in ((qf, wqt, 0.125), (kf, wkt, None), (vf, wvt, None)):
            result = mm(flat, weight[...])
            if scale is not None:
                result = result * scale
            for h in range(pairs):
                target[h, there, :] = result[:, h * 128:(h + 1) * 128]

    def one_agent(a, carry):
        mine = pl.ds(a, total_steps, stride=sub)
        for h in range(pairs):
            query = two_heads(qf[h, mine, :].astype(bf16))
            scores = mm_nt(query, kf[h, mine, :].astype(bf16)) + mask[...]
            weights = jnp.exp(scores - jnp.max(scores, axis=-1, keepdims=True))
            totals = jnp.sum(weights, axis=-1, keepdims=True)
            summed = mm(weights.astype(bf16), vf[h, mine, :].astype(bf16))
            mixed_t[h, mine, :] = join_heads(summed / totals)
        return carry

    lax.fori_loop(0, sub, one_agent, 0)

    second = []
    for k in list(range(1, groups)) + [0]:
        piece = jnp.concatenate([mixed_t[h, pl.ds(k * rows, rows), :] for h in range(pairs)], axis=1).astype(bf16)
        if k == 0:
            recv2[0] = piece
            continue
        send2[k] = piece
        copy = pltpu.make_async_remote_copy(
            src_ref=send2.at[k], dst_ref=recv2.at[k], send_sem=s2.at[k], recv_sem=r2.at[k],
            device_id={"tm": tm_peer(-k)}, device_id_type=MESH,
        )
        copy.start()
        second.append(copy)

    loads[5].wait()
    for g in range(groups // batch):
        for k in range(g * batch, (g + 1) * batch):
            if k:
                second[k - 1].wait_recv()
        added = mm(recv2[g * batch:(g + 1) * batch].reshape(batch * rows, 512), wot[...])
        for k in range(batch):
            base = pl.multiple_of(tm_peer(g * batch + k) * sub, sub)
            for t in range(steps):
                after[t, pl.ds(base, sub), :] = added[(k * steps + t) * sub:(k * steps + t + 1) * sub]
    for t in range(steps):
        both = (wide[t] + after[t]).astype(bf16)
        aft_b[t] = both
        tokens[t] = normed(both.astype(f32))

    third = []

    def send_tokens(target, step, chip, part, j):
        for c in range(2):
            here = pl.ds(c * half, half)
            source = tokens.at[step, here, :]
            destination = target.at[ag, here, :]
            local_copy = pltpu.make_async_copy(source, destination, r3.at[part, ag])
            copy = pltpu.make_async_remote_copy(
                src_ref=source, dst_ref=destination, send_sem=s3.at[part, j, c], recv_sem=r3.at[part, ag],
                device_id={"tm": tm - core + c, "agent": chip}, device_id_type=MESH,
            )
            stays = jnp.logical_and(chip == ag, core == c)
            pl.when(stays)(local_copy.start)
            pl.when(jnp.logical_not(stays))(copy.start)
            third.append((stays, copy))

    for j in range(4):
        step = lax.rem(duo + j, 4)
        send_tokens(all_full, step, 2 * step + core, 0, j)
    for j in range(4):
        turn = lax.rem(ag + j, 4)
        send_tokens(all_part, 4 + turn // 2, 4 * core + turn, 1, j)

    fourth = []
    partner = tm + 1 - 2 * core
    full_order = [2 * lax.rem(full_step - j + 4, 4) + e for j in range(4) for e in range(2)]
    part_order = [lax.rem(ag - j + blocks, 4) + 4 * e for j in range(4) for e in range(2)]

    def hand_over(target, part, order):
        handed = []
        for n, source in enumerate(order):
            here = target.at[source, pl.ds(core * half, half), :]
            pltpu.make_async_copy(here, here, r3.at[part, source]).wait()
            copy = pltpu.make_async_remote_copy(
                src_ref=here, dst_ref=here, send_sem=s4.at[part, n], recv_sem=r4.at[part, n],
                device_id={"tm": partner}, device_id_type=MESH,
            )
            copy.start()
            handed.append(copy)
        fourth.extend(handed)
        return handed

    def project(target, result, weights, order, handed):
        for j in range(4):
            for copy in handed[2 * j:2 * j + 2]:
                copy.wait_recv()
            flat = jnp.concatenate([target[order[2 * j + e]] for e in range(2)], axis=0)
            for n, weight in enumerate(weights):
                made = mm(flat, weight[...])
                if n == 0:
                    made = made * 0.125
                for e in range(2):
                    result[order[2 * j + e], n] = made[e * agents:(e + 1) * agents].astype(bf16)

    fifth = []

    def attention(qkv, ret, many, owner_core, step, lanes, slot, part):
        def one_block(k, carry):
            block = ag_peer(-k)
            near_blocks = [nb_ref[block, j] for j in range(near)]
            for h in range(many):
                columns = slice(h * 128, (h + 1) * 128)
                query = two_heads(qkv[block, 0][:, columns])
                keys = jnp.concatenate([qkv[b, 1][:, columns] for b in near_blocks], axis=0)
                values = jnp.concatenate([qkv[b, 2][:, columns] for b in near_blocks], axis=0)
                scores = mm_nt(query, keys)
                weights = jnp.exp(scores - jnp.max(scores, axis=-1, keepdims=True))
                totals = jnp.sum(weights, axis=-1, keepdims=True)
                summed = mm(weights.astype(bf16), values)
                ret[k, :, columns] = join_heads(summed / totals).astype(bf16)
            return carry

        for k0 in range(0, blocks, 4):
            lax.fori_loop(k0, k0 + 4, one_block, 0)
            for k in range(k0, k0 + 4):
                copy = pltpu.make_async_remote_copy(
                    src_ref=ret.at[k], dst_ref=am.at[step, :, lanes], send_sem=s5.at[part, k],
                    recv_sem=r5.at[step, slot],
                    device_id={"tm": tm - core + owner_core, "agent": ag_peer(-k)}, device_id_type=MESH,
                )
                if k:
                    copy.start()
                    fifth.append((None, copy))
                else:
                    stays = owner_core == core
                    own = pltpu.make_async_copy(ret.at[k], am.at[step, :, lanes], r5.at[step, slot])
                    pl.when(stays)(own.start)
                    pl.when(jnp.logical_not(stays))(copy.start)
                    fifth.append((stays, copy))

    stores = []

    def tail(where):
        for w in where:
            width = 256 if w < 4 else 128
            for slot in range(512 // width):
                target = am.at[w, :, pl.ds(slot * width, width)]
                pltpu.make_async_copy(target, target, r5.at[w, slot]).wait()
        both = jnp.concatenate([am[w] for w in where], axis=0)
        base = jnp.concatenate([aft_b[w] for w in where], axis=0).astype(f32)
        after_agent = (base + mm(both, woa[...])).astype(bf16).astype(f32)
        inner = jax.nn.gelu(mm(normed(after_agent), win[...]), approximate=True).astype(bf16)
        final = (after_agent + mm(inner, wmo[...])).astype(bf16)
        for n, w in enumerate(where):
            outs[w] = final[n * agents:(n + 1) * agents]
            store = pltpu.make_async_copy(outs.at[w], out_hbm.at[w], out_sem.at[w])
            store.start()
            stores.append(store)

    for load in loads[6:12]:
        load.wait()
    handed = hand_over(all_full, 0, full_order)
    project(all_full, qkv_full, (wqa, wka, wva), full_order, handed)
    attention(qkv_full, ret_full, 2, full_core, full_step, full_lanes, core, 0)
    handed = hand_over(all_part, 1, part_order)
    project(all_part, qkv_part, (wqb, wkb, wvb), part_order, handed)
    attention(qkv_part, ret_part, 1, part_core, part_step, part_lanes, side * 2 + core, 1)
    for load in loads[12:]:
        load.wait()
    for w in range(0, steps, 2):
        tail([w, w + 1])

    for copy in first + second + fourth:
        copy.wait_send()
    for stays, copy in third + fifth:
        if stays is None:
            copy.wait_send()
        else:
            pl.when(jnp.logical_not(stays))(copy.wait_send)
    for store in stores:
        store.wait()


def local(
    groups, blocks,
    states, neighbours, w_query_t, w_key_t, w_value_t, w_out_t, w_query_a, w_key_a, w_value_a, w_out_a, w_in, w_mlp_out,
):
    steps, agents, width = states.shape
    hidden = w_in.shape[1]
    rows = steps * (agents // groups)
    total = groups * steps
    square = (width, width)
    anywhere = pl.BlockSpec(memory_space=pl.ANY)
    dma = pltpu.SemaphoreType.DMA
    pieces = pltpu.VMEM((groups, rows, width), bf16)
    by_pair = pltpu.VMEM((width // 128, groups * rows, 128), f32)
    return pl.pallas_call(
        functools.partial(kernel, groups, blocks, steps, agents, neighbours.shape[1]),
        out_shape=jax.ShapeDtypeStruct(states.shape, bf16),
        in_specs=[anywhere] * 12,
        out_specs=anywhere,
        scratch_shapes=[
            pltpu.SMEM(neighbours.shape, jnp.int32),
            pltpu.VMEM(states.shape, bf16),
            pltpu.VMEM(states.shape, f32),
            *[pltpu.VMEM(square, bf16)] * 4,
            *[pltpu.VMEM((width, 256), bf16)] * 3,
            *[pltpu.VMEM((width, 128), bf16)] * 3,
            pltpu.VMEM(square, bf16),
            pltpu.VMEM((width, hidden), bf16),
            pltpu.VMEM((hidden, width), bf16),
            pieces, pieces, by_pair, by_pair, by_pair,
            pltpu.VMEM((2 * total, total), f32),
            by_pair, pieces, pieces,
            pltpu.VMEM(states.shape, f32),
            pltpu.VMEM(states.shape, bf16),
            pltpu.VMEM(states.shape, bf16),
            pltpu.VMEM((blocks, agents, width), bf16),
            pltpu.VMEM((blocks, agents, width), bf16),
            pltpu.VMEM((blocks, 3, agents, 256), bf16),
            pltpu.VMEM((blocks, 3, agents, 128), bf16),
            pltpu.VMEM((blocks, agents, 256), bf16),
            pltpu.VMEM((blocks, agents, 128), bf16),
            pltpu.VMEM(states.shape, bf16),
            pltpu.VMEM(states.shape, bf16),
            dma((15,)), dma((steps,)),
            dma((groups,)), dma((groups,)), dma((groups,)), dma((groups,)),
            dma((2, 4, 2)), dma((2, blocks)),
            dma((2, blocks)), dma((2, blocks)),
            dma((2, blocks)), dma((steps, 4)),
        ],
        compiler_params=pltpu.CompilerParams(
            collective_id=0, has_side_effects=True, vmem_limit_bytes=60 * 1024 * 1024
        ),
    )(states, neighbours, w_query_t, w_key_t, w_value_t, w_out_t, w_query_a, w_key_a, w_value_a, w_out_a, w_in, w_mlp_out)


def solution(mesh):
    placed = (P("tm", "agent", None), P(), P(), P(), P(), P(), P(), P(), P(), P(), P(), P())
    return jax.shard_map(
        functools.partial(local, mesh.shape["tm"], mesh.shape["agent"]),
        mesh=mesh, in_specs=placed, out_specs=P("tm", "agent", None), check_vma=False,
    )
```

```python
import functools

import jax
import jax.numpy as jnp
from jax import lax
from jax.experimental import pallas as pl
from jax.experimental.pallas import tpu as pltpu
from jax.sharding import PartitionSpec as P

MESH = pl.DeviceIdType.MESH
HEADS = 8
epsilon = 1e-06
negative_floor = -1e30
FAR = [1, 2, 3, 4, 5, 6, 7]
THROTTLE = True
bf16 = jnp.bfloat16
f32 = jnp.float32


def normed(wide):
    return (wide * lax.rsqrt(jnp.mean(wide * wide, axis=-1, keepdims=True) + epsilon)).astype(bf16)


def mm(a, b):
    return jnp.dot(a, b, preferred_element_type=f32)


def mm_nt(a, b):
    return lax.dot_general(a, b, (((1,), (1,)), ((), ())), preferred_element_type=f32)


def two_heads(query):
    low = lax.broadcasted_iota(jnp.int32, query.shape, 1) < 64
    none = jnp.zeros_like(query)
    return jnp.concatenate([jnp.where(low, query, none), jnp.where(low, none, query)], axis=0)


def join_heads(stacked):
    n = stacked.shape[0] // 2
    low = lax.broadcasted_iota(jnp.int32, (n, 128), 1) < 64
    return jnp.where(low, stacked[:n], stacked[n:])


def kernel(
    groups, blocks, steps, agents, near,
    states_hbm, nb_hbm, wqt_hbm, wkt_hbm, wvt_hbm, wot_hbm, wqa_hbm, wka_hbm, wva_hbm, woa_hbm, win_hbm, wmo_hbm,
    outs,
    nb_ref, states, wide, wqt, wkt, wvt, wot, wqa, wka, wva, wqb, wkb, wvb, woa, win, wmo,
    send1, recv1, qf, kf, vf, mask, mixed_t, send2, recv2, after, aft_b, tokens, all_full, all_part,
    qkv_full, qkv_part, ret_full, ret_part, am,
    in_sem, s1, r1, s2, r2, s3, r3, s4, r4, s5, r5,
):
    tm = lax.axis_index("tm")
    ag = lax.axis_index("agent")
    core = lax.rem(tm, 2)
    sub = agents // groups
    rows = steps * sub
    pairs = HEADS // 2
    half = agents // 2

    chips = groups // 2
    chip = tm // 2

    def tm_peer(k):
        return lax.rem(tm + k + groups, groups)

    def chip_at(k):
        return lax.rem(chip + k + chips, chips)

    def ag_peer(k):
        return lax.rem(ag + k + blocks, blocks)

    duo, side = ag // 2, lax.rem(ag, 2)
    full_core, full_step = side, duo
    part_core, part_step = duo // 2, 4 + lax.rem(duo, 2)
    full_lanes = pl.ds(pl.multiple_of(core * 256, 256), 256)
    part_lanes = pl.ds(pl.multiple_of((side * 2 + core) * 128, 128), 128)

    sources = [(states_hbm, states), (nb_hbm, nb_ref), (wqt_hbm, wqt), (wkt_hbm, wkt), (wvt_hbm, wvt), (wot_hbm, wot)]
    for hbm, wide_cols, few_cols in ((wqa_hbm, wqa, wqb), (wka_hbm, wka, wkb), (wva_hbm, wva, wvb)):
        sources += [(hbm.at[:, full_lanes], wide_cols), (hbm.at[:, part_lanes], few_cols)]
    sources += [(woa_hbm, woa), (win_hbm, win), (wmo_hbm, wmo)]
    loads = [pltpu.make_async_copy(source, target, in_sem.at[n]) for n, (source, target) in enumerate(sources)]
    loads[0].start()
    barrier = pltpu.get_barrier_semaphore()
    for k in range(1, groups):
        pl.semaphore_signal(barrier, inc=1, device_id={"tm": tm_peer(k)}, device_id_type=MESH)
    for k in range(1, blocks):
        for c in range(2):
            pl.semaphore_signal(
                barrier, inc=1, device_id={"tm": tm - core + c, "agent": ag_peer(k)}, device_id_type=MESH
            )
    for load in loads[1:]:
        load.start()

    loads[0].wait()
    wide[...] = states[...].astype(f32)

    def share(chip_of, c):
        return pl.multiple_of((c * chips + chip_of) * sub, sub)

    for q in range(chips):
        for c in range(2):
            base = share(chip_at(q), c)
            send1[2 * q + c] = jnp.concatenate(
                [wide[t, pl.ds(base, sub), :] for t in range(steps)], axis=0
            ).astype(bf16)
    recv1[core] = send1[core]
    pl.semaphore_wait(barrier, groups - 1 + 2 * (blocks - 1))

    def to_time(q, c):
        return pltpu.make_async_remote_copy(
            src_ref=send1.at[2 * q + c], dst_ref=recv1.at[2 * q + core], send_sem=s1.at[2 * q + c],
            recv_sem=r1.at[2 * q + core], device_id={"tm": 2 * chip_at(q) + c}, device_id_type=MESH,
        )

    early = [to_time(q, 0) for q in FAR]
    late = [to_time(q, 1) for q in FAR]
    beside = to_time(0, 1 - core)
    for copy in early:
        copy.start()
    beside.start()
    for ahead, copy in zip(early, late):
        if THROTTLE:
            ahead.wait_send()
        copy.start()
    unsent = late + [beside] + ([] if THROTTLE else early)

    def arrived(buffer, sems, slot):
        piece = buffer.at[slot]
        pltpu.make_async_copy(piece, piece, sems.at[slot]).wait()

    total_steps = groups * steps

    def times(shape, axis):
        row = lax.broadcasted_iota(jnp.int32, shape, axis).astype(f32)
        row = jnp.where(row >= total_steps, row - total_steps, row)
        slot = jnp.floor((row + 0.5) / steps)
        back = jnp.floor((slot + 0.5) / 2)
        owner = chip.astype(f32) - back
        owner = jnp.where(owner < 0, owner + chips, owner)
        return row + 2 * steps * (owner - back)

    shape = (2 * total_steps, total_steps)
    mask[...] = jnp.where(times(shape, 1) <= times(shape, 0), 0.0, negative_floor)

    for load in loads[1:5]:
        load.wait()
    batch = 4
    for g in range(groups // batch):
        if g == 0:
            arrived(recv1, r1, 1 - core)
        for k in range(max(2, g * batch), (g + 1) * batch):
            arrived(recv1, r1, k)
        there = pl.ds(g * batch * rows, batch * rows)
        flat = normed(recv1[g * batch:(g + 1) * batch].reshape(batch * rows, 512).astype(f32))
        for target, weight, scale in ((qf, wqt, 0.125), (kf, wkt, None), (vf, wvt, None)):
            result = mm(flat, weight[...])
            if scale is not None:
                result = result * scale
            for h in range(pairs):
                target[h, there, :] = result[:, h * 128:(h + 1) * 128]

    def one_agent(a, carry):
        mine = pl.ds(a, total_steps, stride=sub)
        for h in range(pairs):
            query = two_heads(qf[h, mine, :].astype(bf16))
            scores = mm_nt(query, kf[h, mine, :].astype(bf16)) + mask[...]
            weights = jnp.exp(scores - jnp.max(scores, axis=-1, keepdims=True))
            totals = jnp.sum(weights, axis=-1, keepdims=True)
            summed = mm(weights.astype(bf16), vf[h, mine, :].astype(bf16))
            mixed_t[h, mine, :] = join_heads(summed / totals)
        return carry

    lax.fori_loop(0, sub, one_agent, 0)

    def result_of(slot):
        return jnp.concatenate([mixed_t[h, pl.ds(slot * rows, rows), :] for h in range(pairs)], axis=1).astype(bf16)

    def to_owner(q, c):
        return pltpu.make_async_remote_copy(
            src_ref=send2.at[2 * q + c], dst_ref=recv2.at[core * chips + q], send_sem=s2.at[2 * q + c],
            recv_sem=r2.at[core * chips + q], device_id={"tm": 2 * chip_at(-q) + c}, device_id_type=MESH,
        )

    for q in FAR + [0]:
        for c in range(2):
            send2[2 * q + c] = result_of(2 * q + c)
            if q:
                copy = to_owner(q, c)
                copy.start()
                unsent.append(copy)
    copy = to_owner(0, 1 - core)
    copy.start()
    unsent.append(copy)
    recv2[core * chips] = send2[core]

    maybe = []

    def send_tokens(target, step, to_chip, part, j, c):
        here = pl.ds(c * half, half)
        source = tokens.at[step, here, :]
        destination = target.at[ag, here, :]
        local_copy = pltpu.make_async_copy(source, destination, r3.at[part, ag])
        copy = pltpu.make_async_remote_copy(
            src_ref=source, dst_ref=destination, send_sem=s3.at[part, j, c], recv_sem=r3.at[part, ag],
            device_id={"tm": tm - core + c, "agent": to_chip}, device_id_type=MESH,
        )
        stays = jnp.logical_and(to_chip == ag, core == c)
        pl.when(stays)(local_copy.start)
        pl.when(jnp.logical_not(stays))(copy.start)
        maybe.append((stays, copy))

    loads[5].wait()
    for c in range(2):
        for q in range(1, chips):
            arrived(recv2, r2, c * chips + q)

        @pl.when(core != c)
        def _():
            arrived(recv2, r2, c * chips)

        added = mm(recv2[c * chips:(c + 1) * chips].reshape(chips * rows, 512), wot[...])
        for q in range(chips):
            base = share(chip_at(q), c)
            for t in range(steps):
                after[t, pl.ds(base, sub), :] = added[(q * steps + t) * sub:(q * steps + t + 1) * sub]
        here = pl.ds(c * half, half)
        for t in range(steps):
            both = (wide[t, here, :] + after[t, here, :]).astype(bf16)
            aft_b[t, here, :] = both
            tokens[t, here, :] = normed(both.astype(f32))
        for j in range(4):
            step = lax.rem(duo + j, 4)
            send_tokens(all_full, step, 2 * step + core, 0, j, c)
        for j in range(4):
            turn = lax.rem(ag + j, 4)
            send_tokens(all_part, 4 + turn // 2, 4 * core + turn, 1, j, c)

    partner = tm + 1 - 2 * core
    full_order = [2 * lax.rem(full_step - j + 4, 4) + e for j in range(4) for e in range(2)]
    part_order = [lax.rem(ag - j + blocks, 4) + 4 * e for j in range(4) for e in range(2)]

    def hand_over(target, part, source, rows_of):
        here = target.at[source, pl.ds(rows_of * half, half), :]
        return pltpu.make_async_remote_copy(
            src_ref=here, dst_ref=here, send_sem=s4.at[part, source], recv_sem=r4.at[part, source],
            device_id={"tm": partner}, device_id_type=MESH,
        )

    def project(target, part, order, c, result, weights):
        here = pl.ds(c * half, half)
        for j in range(0, blocks, 4):
            for source in order[j:j + 4]:
                copy = hand_over(target, part, source, c)

                @pl.when(core == c)
                def _():
                    piece = target.at[source, here, :]
                    pltpu.make_async_copy(piece, piece, r3.at[part, source]).wait()
                    copy.start()

                @pl.when(core != c)
                def _():
                    copy.wait_recv()

            flat = jnp.concatenate([target[source, here, :] for source in order[j:j + 4]], axis=0)
            for n, weight in enumerate(weights):
                made = mm(flat, weight[...])
                if n == 0:
                    made = made * 0.125
                for e, source in enumerate(order[j:j + 4]):
                    result[source, n, here, :] = made[e * half:(e + 1) * half].astype(bf16)

    fifth = []

    def attention(qkv, ret, many, owner_core, step, lanes, slot, part):
        def one_block(k, carry):
            block = ag_peer(-k)
            near_blocks = [nb_ref[j, block] for j in range(near)]
            for h in range(many):
                columns = slice(h * 128, (h + 1) * 128)
                query = two_heads(qkv[block, 0][:, columns])
                keys = jnp.concatenate([qkv[b, 1][:, columns] for b in near_blocks], axis=0)
                values = jnp.concatenate([qkv[b, 2][:, columns] for b in near_blocks], axis=0)
                scores = mm_nt(query, keys)
                weights = jnp.exp(scores - jnp.max(scores, axis=-1, keepdims=True))
                totals = jnp.sum(weights, axis=-1, keepdims=True)
                summed = mm(weights.astype(bf16), values)
                ret[k, :, columns] = join_heads(summed / totals).astype(bf16)
            return carry

        for k0 in range(0, blocks, 4):
            lax.fori_loop(k0, k0 + 4, one_block, 0)
            for k in range(k0, k0 + 4):
                copy = pltpu.make_async_remote_copy(
                    src_ref=ret.at[k], dst_ref=am.at[step, :, lanes], send_sem=s5.at[part, k],
                    recv_sem=r5.at[step, slot],
                    device_id={"tm": tm - core + owner_core, "agent": ag_peer(-k)}, device_id_type=MESH,
                )
                if k:
                    copy.start()
                    fifth.append((None, copy))
                else:
                    stays = owner_core == core
                    own = pltpu.make_async_copy(ret.at[k], am.at[step, :, lanes], r5.at[step, slot])
                    pl.when(stays)(own.start)
                    pl.when(jnp.logical_not(stays))(copy.start)
                    fifth.append((stays, copy))

    def tail(where):
        for w in where:
            width = 256 if w < 4 else 128
            for slot in range(512 // width):
                target = am.at[w, :, pl.ds(slot * width, width)]
                pltpu.make_async_copy(target, target, r5.at[w, slot]).wait()
        both = jnp.concatenate([am[w] for w in where], axis=0)
        base = jnp.concatenate([aft_b[w] for w in where], axis=0).astype(f32)
        after_agent = (base + mm(both, woa[...])).astype(bf16).astype(f32)
        inner = jax.nn.gelu(mm(normed(after_agent), win[...]), approximate=True).astype(bf16)
        final = (after_agent + mm(inner, wmo[...])).astype(bf16)
        for n, w in enumerate(where):
            outs[w] = final[n * agents:(n + 1) * agents]

    for load in loads[6:12]:
        load.wait()
    of_full = (all_full, 0, full_order)
    of_part = (all_part, 1, part_order)
    project(*of_full, 0, qkv_full, (wqa, wka, wva))
    project(*of_part, 0, qkv_part, (wqb, wkb, wvb))
    project(*of_full, 1, qkv_full, (wqa, wka, wva))
    attention(qkv_full, ret_full, 2, full_core, full_step, full_lanes, core, 0)
    project(*of_part, 1, qkv_part, (wqb, wkb, wvb))
    attention(qkv_part, ret_part, 1, part_core, part_step, part_lanes, side * 2 + core, 1)
    for load in loads[12:]:
        load.wait()
    for w in range(0, steps, 2):
        tail([w, w + 1])

    for copy in unsent:
        copy.wait_send()
    for source in range(blocks):
        for part, target in ((0, all_full), (1, all_part)):
            hand_over(target, part, source, core).wait_send()
    for stays, copy in maybe + fifth:
        if stays is None:
            copy.wait_send()
        else:
            pl.when(jnp.logical_not(stays))(copy.wait_send)


def local(
    groups, blocks,
    states, neighbours, w_query_t, w_key_t, w_value_t, w_out_t, w_query_a, w_key_a, w_value_a, w_out_a, w_in, w_mlp_out,
):
    steps, agents, width = states.shape
    hidden = w_in.shape[1]
    rows = steps * (agents // groups)
    total = groups * steps
    square = (width, width)
    anywhere = pl.BlockSpec(memory_space=pl.ANY)
    dma = pltpu.SemaphoreType.DMA
    pieces = pltpu.VMEM((groups, rows, width), bf16)
    by_pair = pltpu.VMEM((width // 128, groups * rows, 128), f32)
    return pl.pallas_call(
        functools.partial(kernel, groups, blocks, steps, agents, neighbours.shape[1]),
        out_shape=pltpu.VMEM(states.shape, bf16),
        in_specs=[anywhere] * 12,
        out_specs=pl.BlockSpec(memory_space=pltpu.VMEM),
        scratch_shapes=[
            pltpu.SMEM(neighbours.shape[::-1], jnp.int32),
            pltpu.VMEM(states.shape, bf16),
            pltpu.VMEM(states.shape, f32),
            *[pltpu.VMEM(square, bf16)] * 4,
            *[pltpu.VMEM((width, 256), bf16)] * 3,
            *[pltpu.VMEM((width, 128), bf16)] * 3,
            pltpu.VMEM(square, bf16),
            pltpu.VMEM((width, hidden), bf16),
            pltpu.VMEM((hidden, width), bf16),
            pieces, pieces, by_pair, by_pair, by_pair,
            pltpu.VMEM((2 * total, total), f32),
            by_pair, pieces, pieces,
            pltpu.VMEM(states.shape, f32),
            pltpu.VMEM(states.shape, bf16),
            pltpu.VMEM(states.shape, bf16),
            pltpu.VMEM((blocks, agents, width), bf16),
            pltpu.VMEM((blocks, agents, width), bf16),
            pltpu.VMEM((blocks, 3, agents, 256), bf16),
            pltpu.VMEM((blocks, 3, agents, 128), bf16),
            pltpu.VMEM((blocks, agents, 256), bf16),
            pltpu.VMEM((blocks, agents, 128), bf16),
            pltpu.VMEM(states.shape, bf16),
            dma((15,)),
            dma((groups,)), dma((groups,)), dma((groups,)), dma((groups,)),
            dma((2, 4, 2)), dma((2, blocks)),
            dma((2, blocks)), dma((2, blocks)),
            dma((2, blocks)), dma((steps, 4)),
        ],
        compiler_params=pltpu.CompilerParams(
            collective_id=0, has_side_effects=True, vmem_limit_bytes=60 * 1024 * 1024
        ),
    )(states, neighbours.T, w_query_t, w_key_t, w_value_t, w_out_t, w_query_a, w_key_a, w_value_a, w_out_a, w_in, w_mlp_out)


def solution(mesh):
    placed = (P("tm", "agent", None), P(), P(), P(), P(), P(), P(), P(), P(), P(), P(), P())
    return jax.shard_map(
        functools.partial(local, mesh.shape["tm"], mesh.shape["agent"]),
        mesh=mesh, in_specs=placed, out_specs=P("tm", "agent", None), check_vma=False,
    )
```

```python
import functools

import jax
import jax.numpy as jnp
from jax import lax
from jax.experimental import pallas as pl
from jax.experimental.pallas import tpu as pltpu
from jax.sharding import PartitionSpec as P

MESH = pl.DeviceIdType.MESH
HEADS = 8
epsilon = 1e-06
negative_floor = -1e30
FAR = [4, 5, 3, 2, 6, 7, 1]
bf16 = jnp.bfloat16
f32 = jnp.float32


def normed(wide):
    return (wide * lax.rsqrt(jnp.mean(wide * wide, axis=-1, keepdims=True) + epsilon)).astype(bf16)


def mm(a, b):
    return jnp.dot(a, b, preferred_element_type=f32)


def mm_nt(a, b):
    return lax.dot_general(a, b, (((1,), (1,)), ((), ())), preferred_element_type=f32)


def two_heads(query):
    low = lax.broadcasted_iota(jnp.int32, query.shape, 1) < 64
    none = jnp.zeros_like(query)
    return jnp.concatenate([jnp.where(low, query, none), jnp.where(low, none, query)], axis=0)


def join_heads(stacked):
    n = stacked.shape[0] // 2
    low = lax.broadcasted_iota(jnp.int32, (n, 128), 1) < 64
    return jnp.where(low, stacked[:n], stacked[n:])


def kernel(
    groups, blocks, steps, agents, near,
    states_hbm, nb_hbm, wqt_hbm, wkt_hbm, wvt_hbm, wot_hbm, wqa_hbm, wka_hbm, wva_hbm, woa_hbm, win_hbm, wmo_hbm,
    outs,
    nb_ref, states, wide, wqt, wkt, wvt, wot, wqa, wka, wva, wqb, wkb, wvb, woa, win, wmo,
    send1, recv1, qf, kf, vf, mask, mixed_t, send2, recv2, after, aft_b, tokens, all_full, all_part,
    qkv_full, qkv_part, ret_full, ret_part, am,
    in_sem, s1, r1, s2, r2, s3, r3, s4, r4, s5, r5,
):
    tm = lax.axis_index("tm")
    ag = lax.axis_index("agent")
    core = lax.rem(tm, 2)
    sub = agents // groups
    rows = steps * sub
    pairs = HEADS // 2
    half = agents // 2

    chips = groups // 2
    chip = tm // 2

    def tm_peer(k):
        return lax.rem(tm + k + groups, groups)

    def chip_at(k):
        return lax.rem(chip + k + chips, chips)

    def ag_peer(k):
        return lax.rem(ag + k + blocks, blocks)

    duo, side = ag // 2, lax.rem(ag, 2)
    full_core, full_step = side, duo
    part_core, part_step = duo // 2, 4 + lax.rem(duo, 2)
    full_lanes = pl.ds(pl.multiple_of(core * 256, 256), 256)
    part_lanes = pl.ds(pl.multiple_of((side * 2 + core) * 128, 128), 128)

    sources = [(states_hbm, states), (nb_hbm, nb_ref), (wqt_hbm, wqt), (wkt_hbm, wkt), (wvt_hbm, wvt), (wot_hbm, wot)]
    for hbm, wide_cols, few_cols in ((wqa_hbm, wqa, wqb), (wka_hbm, wka, wkb), (wva_hbm, wva, wvb)):
        sources += [(hbm.at[:, full_lanes], wide_cols), (hbm.at[:, part_lanes], few_cols)]
    sources += [(woa_hbm, woa), (win_hbm, win), (wmo_hbm, wmo)]
    loads = [pltpu.make_async_copy(source, target, in_sem.at[n]) for n, (source, target) in enumerate(sources)]
    loads[0].start()
    barrier = pltpu.get_barrier_semaphore()
    for k in range(1, groups):
        pl.semaphore_signal(barrier, inc=1, device_id={"tm": tm_peer(k)}, device_id_type=MESH)
    for k in range(1, blocks):
        for c in range(2):
            pl.semaphore_signal(
                barrier, inc=1, device_id={"tm": tm - core + c, "agent": ag_peer(k)}, device_id_type=MESH
            )
    for load in loads[1:]:
        load.start()

    loads[0].wait()
    wide[...] = states[...].astype(f32)

    def share(chip_of, c):
        return pl.multiple_of((c * chips + chip_of) * sub, sub)

    for q in range(chips):
        for c in range(2):
            base = share(chip_at(q), c)
            send1[2 * q + c] = jnp.concatenate(
                [wide[t, pl.ds(base, sub), :] for t in range(steps)], axis=0
            ).astype(bf16)
    recv1[core] = send1[core]
    pl.semaphore_wait(barrier, groups - 1 + 2 * (blocks - 1))

    def to_time(q, c):
        return pltpu.make_async_remote_copy(
            src_ref=send1.at[2 * q + c], dst_ref=recv1.at[2 * q + core], send_sem=s1.at[2 * q + c],
            recv_sem=r1.at[2 * q + core], device_id={"tm": 2 * chip_at(q) + c}, device_id_type=MESH,
        )

    early = [to_time(q, 0) for q in FAR]
    late = [to_time(q, 1) for q in FAR]
    beside = to_time(0, 1 - core)
    for copy in early:
        copy.start()
    beside.start()
    for ahead, copy in zip(early, late):
        ahead.wait_send()
        copy.start()
    unsent = late + [beside]

    def arrived(buffer, sems, slot):
        piece = buffer.at[slot]
        pltpu.make_async_copy(piece, piece, sems.at[slot]).wait()

    total_steps = groups * steps

    def times(shape, axis):
        row = lax.broadcasted_iota(jnp.int32, shape, axis).astype(f32)
        row = jnp.where(row >= total_steps, row - total_steps, row)
        slot = jnp.floor((row + 0.5) / steps)
        back = jnp.floor((slot + 0.5) / 2)
        owner = chip.astype(f32) - back
        owner = jnp.where(owner < 0, owner + chips, owner)
        return row + 2 * steps * (owner - back)

    shape = (2 * total_steps, total_steps)
    mask[...] = jnp.where(times(shape, 1) <= times(shape, 0), 0.0, negative_floor)

    for load in loads[1:5]:
        load.wait()
    batch = 4
    for g in range(groups // batch):
        if g == 0:
            arrived(recv1, r1, 1 - core)
        for k in range(max(2, g * batch), (g + 1) * batch):
            arrived(recv1, r1, k)
        there = pl.ds(g * batch * rows, batch * rows)
        flat = normed(recv1[g * batch:(g + 1) * batch].reshape(batch * rows, 512).astype(f32))
        for target, weight, scale in ((qf, wqt, 0.125), (kf, wkt, None), (vf, wvt, None)):
            result = mm(flat, weight[...])
            if scale is not None:
                result = result * scale
            for h in range(pairs):
                target[h, there, :] = result[:, h * 128:(h + 1) * 128]

    def one_agent(a, carry):
        mine = pl.ds(a, total_steps, stride=sub)
        for h in range(pairs):
            query = two_heads(qf[h, mine, :].astype(bf16))
            scores = mm_nt(query, kf[h, mine, :].astype(bf16)) + mask[...]
            weights = jnp.exp(scores - jnp.max(scores, axis=-1, keepdims=True))
            totals = jnp.sum(weights, axis=-1, keepdims=True)
            summed = mm(weights.astype(bf16), vf[h, mine, :].astype(bf16))
            mixed_t[h, mine, :] = join_heads(summed / totals)
        return carry

    lax.fori_loop(0, sub, one_agent, 0, unroll=4)

    def result_of(slot):
        return jnp.concatenate([mixed_t[h, pl.ds(slot * rows, rows), :] for h in range(pairs)], axis=1).astype(bf16)

    def to_owner(q, c):
        return pltpu.make_async_remote_copy(
            src_ref=send2.at[2 * q + c], dst_ref=recv2.at[core * chips + q], send_sem=s2.at[2 * q + c],
            recv_sem=r2.at[core * chips + q], device_id={"tm": 2 * chip_at(-q) + c}, device_id_type=MESH,
        )

    for q in FAR + [0]:
        for c in range(2):
            send2[2 * q + c] = result_of(2 * q + c)
            if q:
                copy = to_owner(q, c)
                copy.start()
                unsent.append(copy)
    copy = to_owner(0, 1 - core)
    copy.start()
    unsent.append(copy)
    recv2[core * chips] = send2[core]

    maybe = []

    def send_tokens(target, step, to_chip, part, j, c):
        here = pl.ds(c * half, half)
        source = tokens.at[step, here, :]
        destination = target.at[ag, here, :]
        local_copy = pltpu.make_async_copy(source, destination, r3.at[part, ag])
        copy = pltpu.make_async_remote_copy(
            src_ref=source, dst_ref=destination, send_sem=s3.at[part, j, c], recv_sem=r3.at[part, ag],
            device_id={"tm": tm - core + c, "agent": to_chip}, device_id_type=MESH,
        )
        stays = jnp.logical_and(to_chip == ag, core == c)
        pl.when(stays)(local_copy.start)
        pl.when(jnp.logical_not(stays))(copy.start)
        maybe.append((stays, copy))

    loads[5].wait()
    for c in range(2):
        for q in range(1, chips):
            arrived(recv2, r2, c * chips + q)

        @pl.when(core != c)
        def _():
            arrived(recv2, r2, c * chips)

        added = mm(recv2[c * chips:(c + 1) * chips].reshape(chips * rows, 512), wot[...])
        for q in range(chips):
            base = share(chip_at(q), c)
            for t in range(steps):
                after[t, pl.ds(base, sub), :] = added[(q * steps + t) * sub:(q * steps + t + 1) * sub]
        here = pl.ds(c * half, half)
        for t in range(steps):
            both = (wide[t, here, :] + after[t, here, :]).astype(bf16)
            aft_b[t, here, :] = both
            tokens[t, here, :] = normed(both.astype(f32))
        for j in range(4):
            step = lax.rem(duo + j, 4)
            send_tokens(all_full, step, 2 * step + core, 0, j, c)
        for j in range(4):
            turn = lax.rem(ag + j, 4)
            send_tokens(all_part, 4 + turn // 2, 4 * core + turn, 1, j, c)

    partner = tm + 1 - 2 * core
    full_order = [2 * lax.rem(full_step - j + 4, 4) + e for j in range(4) for e in range(2)]
    part_order = [lax.rem(ag - j + blocks, 4) + 4 * e for j in range(4) for e in range(2)]

    def hand_over(target, part, source, rows_of):
        here = target.at[source, pl.ds(rows_of * half, half), :]
        return pltpu.make_async_remote_copy(
            src_ref=here, dst_ref=here, send_sem=s4.at[part, source], recv_sem=r4.at[part, source],
            device_id={"tm": partner}, device_id_type=MESH,
        )

    def project(target, part, order, c, result, weights):
        here = pl.ds(c * half, half)
        for j in range(0, blocks, 4):
            for source in order[j:j + 4]:
                copy = hand_over(target, part, source, c)

                @pl.when(core == c)
                def _():
                    piece = target.at[source, here, :]
                    pltpu.make_async_copy(piece, piece, r3.at[part, source]).wait()
                    copy.start()

                @pl.when(core != c)
                def _():
                    copy.wait_recv()

            flat = jnp.concatenate([target[source, here, :] for source in order[j:j + 4]], axis=0)
            for n, weight in enumerate(weights):
                made = mm(flat, weight[...])
                if n == 0:
                    made = made * 0.125
                for e, source in enumerate(order[j:j + 4]):
                    result[source, n, here, :] = made[e * half:(e + 1) * half].astype(bf16)

    fifth = []

    def attention(qkv, ret, many, owner_core, step, lanes, slot, part):
        def one_block(k, carry):
            block = ag_peer(-k)
            near_blocks = [nb_ref[j, block] for j in range(near)]
            for h in range(many):
                columns = slice(h * 128, (h + 1) * 128)
                query = two_heads(qkv[block, 0][:, columns])
                keys = jnp.concatenate([qkv[b, 1][:, columns] for b in near_blocks], axis=0)
                values = jnp.concatenate([qkv[b, 2][:, columns] for b in near_blocks], axis=0)
                scores = mm_nt(query, keys)
                weights = jnp.exp(scores - jnp.max(scores, axis=-1, keepdims=True))
                totals = jnp.sum(weights, axis=-1, keepdims=True)
                summed = mm(weights.astype(bf16), values)
                ret[k, :, columns] = join_heads(summed / totals).astype(bf16)
            return carry

        for k0 in range(0, blocks, 2):
            lax.fori_loop(k0, k0 + 2, one_block, 0, unroll=2)
            for k in range(k0, k0 + 2):
                copy = pltpu.make_async_remote_copy(
                    src_ref=ret.at[k], dst_ref=am.at[step, :, lanes], send_sem=s5.at[part, k],
                    recv_sem=r5.at[step, slot],
                    device_id={"tm": tm - core + owner_core, "agent": ag_peer(-k)}, device_id_type=MESH,
                )
                if k:
                    copy.start()
                    fifth.append((None, copy))
                else:
                    stays = owner_core == core
                    own = pltpu.make_async_copy(ret.at[k], am.at[step, :, lanes], r5.at[step, slot])
                    pl.when(stays)(own.start)
                    pl.when(jnp.logical_not(stays))(copy.start)
                    fifth.append((stays, copy))

    def tail(where):
        for w in where:
            width = 256 if w < 4 else 128
            for slot in range(512 // width):
                target = am.at[w, :, pl.ds(slot * width, width)]
                pltpu.make_async_copy(target, target, r5.at[w, slot]).wait()
        both = jnp.concatenate([am[w] for w in where], axis=0)
        base = jnp.concatenate([aft_b[w] for w in where], axis=0).astype(f32)
        after_agent = (base + mm(both, woa[...])).astype(bf16).astype(f32)
        inner = jax.nn.gelu(mm(normed(after_agent), win[...]), approximate=True).astype(bf16)
        final = (after_agent + mm(inner, wmo[...])).astype(bf16)
        for n, w in enumerate(where):
            outs[w] = final[n * agents:(n + 1) * agents]

    for load in loads[6:12]:
        load.wait()
    of_full = (all_full, 0, full_order)
    of_part = (all_part, 1, part_order)
    project(*of_full, 0, qkv_full, (wqa, wka, wva))
    project(*of_part, 0, qkv_part, (wqb, wkb, wvb))
    project(*of_full, 1, qkv_full, (wqa, wka, wva))
    attention(qkv_full, ret_full, 2, full_core, full_step, full_lanes, core, 0)
    project(*of_part, 1, qkv_part, (wqb, wkb, wvb))
    attention(qkv_part, ret_part, 1, part_core, part_step, part_lanes, side * 2 + core, 1)
    for load in loads[12:]:
        load.wait()
    for w in range(0, steps, 2):
        tail([w, w + 1])

    for copy in unsent:
        copy.wait_send()
    for source in range(blocks):
        for part, target in ((0, all_full), (1, all_part)):
            hand_over(target, part, source, core).wait_send()
    for stays, copy in maybe + fifth:
        if stays is None:
            copy.wait_send()
        else:
            pl.when(jnp.logical_not(stays))(copy.wait_send)


def local(
    groups, blocks,
    states, neighbours, w_query_t, w_key_t, w_value_t, w_out_t, w_query_a, w_key_a, w_value_a, w_out_a, w_in, w_mlp_out,
):
    steps, agents, width = states.shape
    hidden = w_in.shape[1]
    rows = steps * (agents // groups)
    total = groups * steps
    square = (width, width)
    anywhere = pl.BlockSpec(memory_space=pl.ANY)
    dma = pltpu.SemaphoreType.DMA
    pieces = pltpu.VMEM((groups, rows, width), bf16)
    by_pair = pltpu.VMEM((width // 128, groups * rows, 128), f32)
    return pl.pallas_call(
        functools.partial(kernel, groups, blocks, steps, agents, neighbours.shape[1]),
        out_shape=pltpu.VMEM(states.shape, bf16),
        in_specs=[anywhere] * 12,
        out_specs=pl.BlockSpec(memory_space=pltpu.VMEM),
        scratch_shapes=[
            pltpu.SMEM(neighbours.shape[::-1], jnp.int32),
            pltpu.VMEM(states.shape, bf16),
            pltpu.VMEM(states.shape, f32),
            *[pltpu.VMEM(square, bf16)] * 4,
            *[pltpu.VMEM((width, 256), bf16)] * 3,
            *[pltpu.VMEM((width, 128), bf16)] * 3,
            pltpu.VMEM(square, bf16),
            pltpu.VMEM((width, hidden), bf16),
            pltpu.VMEM((hidden, width), bf16),
            pieces, pieces, by_pair, by_pair, by_pair,
            pltpu.VMEM((2 * total, total), f32),
            by_pair, pieces, pieces,
            pltpu.VMEM(states.shape, f32),
            pltpu.VMEM(states.shape, bf16),
            pltpu.VMEM(states.shape, bf16),
            pltpu.VMEM((blocks, agents, width), bf16),
            pltpu.VMEM((blocks, agents, width), bf16),
            pltpu.VMEM((blocks, 3, agents, 256), bf16),
            pltpu.VMEM((blocks, 3, agents, 128), bf16),
            pltpu.VMEM((blocks, agents, 256), bf16),
            pltpu.VMEM((blocks, agents, 128), bf16),
            pltpu.VMEM(states.shape, bf16),
            dma((15,)),
            dma((groups,)), dma((groups,)), dma((groups,)), dma((groups,)),
            dma((2, 4, 2)), dma((2, blocks)),
            dma((2, blocks)), dma((2, blocks)),
            dma((2, blocks)), dma((steps, 4)),
        ],
        compiler_params=pltpu.CompilerParams(
            collective_id=0, has_side_effects=True, vmem_limit_bytes=60 * 1024 * 1024
        ),
    )(states, neighbours.T, w_query_t, w_key_t, w_value_t, w_out_t, w_query_a, w_key_a, w_value_a, w_out_a, w_in, w_mlp_out)


def solution(mesh):
    placed = (P("tm", "agent", None), P(), P(), P(), P(), P(), P(), P(), P(), P(), P(), P())
    return jax.shard_map(
        functools.partial(local, mesh.shape["tm"], mesh.shape["agent"]),
        mesh=mesh, in_specs=placed, out_specs=P("tm", "agent", None), check_vma=False,
    )
```

```python
import functools

import jax
import jax.numpy as jnp
from jax import lax
from jax.experimental import pallas as pl
from jax.experimental.pallas import tpu as pltpu
from jax.sharding import PartitionSpec as P

MESH = pl.DeviceIdType.MESH
HEADS = 8
epsilon = 1e-06
negative_floor = -1e30
FAR = [4, 5, 3, 2, 6, 7, 1]
bf16 = jnp.bfloat16
f32 = jnp.float32


def normed(wide):
    return (wide * lax.rsqrt(jnp.mean(wide * wide, axis=-1, keepdims=True) + epsilon)).astype(bf16)


def mm(a, b):
    return jnp.dot(a, b, preferred_element_type=f32)


def mm_nt(a, b):
    return lax.dot_general(a, b, (((1,), (1,)), ((), ())), preferred_element_type=f32)


def two_heads(query):
    low = lax.broadcasted_iota(jnp.int32, query.shape, 1) < 64
    none = jnp.zeros_like(query)
    return jnp.concatenate([jnp.where(low, query, none), jnp.where(low, none, query)], axis=0)


def join_heads(stacked):
    n = stacked.shape[0] // 2
    low = lax.broadcasted_iota(jnp.int32, (n, 128), 1) < 64
    return jnp.where(low, stacked[:n], stacked[n:])


def kernel(
    groups, blocks, steps, agents, near,
    states_hbm, nb_hbm, wqt_hbm, wkt_hbm, wvt_hbm, wot_hbm, wqa_hbm, wka_hbm, wva_hbm, woa_hbm, win_hbm, wmo_hbm,
    outs,
    nb_ref, states, wide, wqt, wkt, wvt, wot, wqa, wka, wva, wqb, wkb, wvb, woa, win, wmo,
    send1, recv1, qf, kf, vf, mask, mixed_t, send2, recv2, after, aft_b, tokens, all_full, all_part,
    qkv_full, qkv_part, ret_full, ret_part, am,
    in_sem, s1, r1, s2, r2, s3, r3, s4, r4, s5, r5,
):
    tm = lax.axis_index("tm")
    ag = lax.axis_index("agent")
    core = lax.rem(tm, 2)
    sub = agents // groups
    rows = steps * sub
    pairs = HEADS // 2
    half = agents // 2

    chips = groups // 2
    chip = tm // 2

    def tm_peer(k):
        return lax.rem(tm + k + groups, groups)

    def chip_at(k):
        return lax.rem(chip + k + chips, chips)

    def ag_peer(k):
        return lax.rem(ag + k + blocks, blocks)

    duo, side = ag // 2, lax.rem(ag, 2)
    full_core, full_step = side, duo
    part_core, part_step = duo // 2, 4 + lax.rem(duo, 2)
    full_lanes = pl.ds(pl.multiple_of(core * 256, 256), 256)
    part_lanes = pl.ds(pl.multiple_of((side * 2 + core) * 128, 128), 128)

    sources = [(states_hbm, states), (nb_hbm, nb_ref), (wqt_hbm, wqt), (wkt_hbm, wkt), (wvt_hbm, wvt), (wot_hbm, wot)]
    for hbm, wide_cols, few_cols in ((wqa_hbm, wqa, wqb), (wka_hbm, wka, wkb), (wva_hbm, wva, wvb)):
        sources += [(hbm.at[:, full_lanes], wide_cols), (hbm.at[:, part_lanes], few_cols)]
    sources += [(woa_hbm, woa), (win_hbm, win), (wmo_hbm, wmo)]
    loads = [pltpu.make_async_copy(source, target, in_sem.at[n]) for n, (source, target) in enumerate(sources)]
    loads[0].start()
    barrier = pltpu.get_barrier_semaphore()
    for k in range(1, groups):
        pl.semaphore_signal(barrier, inc=1, device_id={"tm": tm_peer(k)}, device_id_type=MESH)
    for k in range(1, blocks):
        for c in range(2):
            pl.semaphore_signal(
                barrier, inc=1, device_id={"tm": tm - core + c, "agent": ag_peer(k)}, device_id_type=MESH
            )
    for load in loads[1:]:
        load.start()

    loads[0].wait()
    wide[...] = states[...].astype(f32)

    def share(chip_of, c):
        return pl.multiple_of((c * chips + chip_of) * sub, sub)

    for q in range(chips):
        for c in range(2):
            base = share(chip_at(q), c)
            send1[2 * q + c] = jnp.concatenate(
                [wide[t, pl.ds(base, sub), :] for t in range(steps)], axis=0
            ).astype(bf16)
    recv1[core] = send1[core]
    pl.semaphore_wait(barrier, groups - 1 + 2 * (blocks - 1))

    def to_time(q, c):
        return pltpu.make_async_remote_copy(
            src_ref=send1.at[2 * q + c], dst_ref=recv1.at[2 * q + core], send_sem=s1.at[2 * q + c],
            recv_sem=r1.at[2 * q + core], device_id={"tm": 2 * chip_at(q) + c}, device_id_type=MESH,
        )

    early = [to_time(q, 0) for q in FAR]
    late = [to_time(q, 1) for q in FAR]
    beside = to_time(0, 1 - core)
    for copy in early:
        copy.start()
    beside.start()
    for ahead, copy in zip(early, late):
        ahead.wait_send()
        copy.start()
    unsent = late + [beside]

    def arrived(buffer, sems, slot):
        piece = buffer.at[slot]
        pltpu.make_async_copy(piece, piece, sems.at[slot]).wait()

    total_steps = groups * steps

    def times(shape, axis):
        row = lax.broadcasted_iota(jnp.int32, shape, axis).astype(f32)
        row = jnp.where(row >= total_steps, row - total_steps, row)
        slot = jnp.floor((row + 0.5) / steps)
        back = jnp.floor((slot + 0.5) / 2)
        owner = chip.astype(f32) - back
        owner = jnp.where(owner < 0, owner + chips, owner)
        return row + 2 * steps * (owner - back)

    shape = (2 * total_steps, total_steps)
    mask[...] = jnp.where(times(shape, 1) <= times(shape, 0), 0.0, negative_floor)

    for load in loads[1:5]:
        load.wait()
    batch = 4
    for g in range(groups // batch):
        if g == 0:
            arrived(recv1, r1, 1 - core)
        for k in range(max(2, g * batch), (g + 1) * batch):
            arrived(recv1, r1, k)
        there = pl.ds(g * batch * rows, batch * rows)
        flat = normed(recv1[g * batch:(g + 1) * batch].reshape(batch * rows, 512).astype(f32))
        for target, weight, scale in ((qf, wqt, 0.125), (kf, wkt, None), (vf, wvt, None)):
            result = mm(flat, weight[...])
            if scale is not None:
                result = result * scale
            for h in range(pairs):
                target[h, there, :] = result[:, h * 128:(h + 1) * 128]

    def one_agent(a, carry):
        mine = pl.ds(a, total_steps, stride=sub)
        for h in range(pairs):
            query = two_heads(qf[h, mine, :].astype(bf16))
            scores = mm_nt(query, kf[h, mine, :].astype(bf16)) + mask[...]
            weights = jnp.exp(scores - jnp.max(scores, axis=-1, keepdims=True))
            totals = jnp.sum(weights, axis=-1, keepdims=True)
            summed = mm(weights.astype(bf16), vf[h, mine, :].astype(bf16))
            mixed_t[h, mine, :] = join_heads(summed / totals)
        return carry

    lax.fori_loop(0, sub, one_agent, 0, unroll=4)

    def result_of(slot):
        return jnp.concatenate([mixed_t[h, pl.ds(slot * rows, rows), :] for h in range(pairs)], axis=1).astype(bf16)

    def to_owner(q, c):
        return pltpu.make_async_remote_copy(
            src_ref=send2.at[2 * q + c], dst_ref=recv2.at[core * chips + q], send_sem=s2.at[2 * q + c],
            recv_sem=r2.at[core * chips + q], device_id={"tm": 2 * chip_at(-q) + c}, device_id_type=MESH,
        )

    for q in FAR + [0]:
        for c in range(2):
            send2[2 * q + c] = result_of(2 * q + c)
            if q:
                copy = to_owner(q, c)
                copy.start()
                unsent.append(copy)
    copy = to_owner(0, 1 - core)
    copy.start()
    unsent.append(copy)
    recv2[core * chips] = send2[core]

    maybe = []

    def send_tokens(target, step, to_chip, part, j, c):
        here = pl.ds(c * half, half)
        source = tokens.at[step, here, :]
        destination = target.at[ag, here, :]
        local_copy = pltpu.make_async_copy(source, destination, r3.at[part, ag])
        copy = pltpu.make_async_remote_copy(
            src_ref=source, dst_ref=destination, send_sem=s3.at[part, j, c], recv_sem=r3.at[part, ag],
            device_id={"tm": tm - core + c, "agent": to_chip}, device_id_type=MESH,
        )
        stays = jnp.logical_and(to_chip == ag, core == c)
        pl.when(stays)(local_copy.start)
        pl.when(jnp.logical_not(stays))(copy.start)
        maybe.append((stays, copy))

    loads[5].wait()
    for c in range(2):
        for q in range(1, chips):
            arrived(recv2, r2, c * chips + q)

        @pl.when(core != c)
        def _():
            arrived(recv2, r2, c * chips)

        added = mm(recv2[c * chips:(c + 1) * chips].reshape(chips * rows, 512), wot[...])
        for q in range(chips):
            base = share(chip_at(q), c)
            for t in range(steps):
                after[t, pl.ds(base, sub), :] = added[(q * steps + t) * sub:(q * steps + t + 1) * sub]
        here = pl.ds(c * half, half)
        for t in range(steps):
            both = (wide[t, here, :] + after[t, here, :]).astype(bf16)
            aft_b[t, here, :] = both
            tokens[t, here, :] = normed(both.astype(f32))
        for j in range(4):
            step = lax.rem(duo + j, 4)
            send_tokens(all_full, step, 2 * step + core, 0, j, c)
        for j in range(4):
            turn = lax.rem(ag + j, 4)
            send_tokens(all_part, 4 + turn // 2, 4 * core + turn, 1, j, c)

    partner = tm + 1 - 2 * core
    full_order = [2 * lax.rem(full_step - j + 4, 4) + e for j in range(4) for e in range(2)]
    part_order = [lax.rem(ag - j + blocks, 4) + 4 * e for j in range(4) for e in range(2)]

    def hand_over(target, part, source, rows_of):
        here = target.at[source, pl.ds(rows_of * half, half), :]
        return pltpu.make_async_remote_copy(
            src_ref=here, dst_ref=here, send_sem=s4.at[part, source], recv_sem=r4.at[part, source],
            device_id={"tm": partner}, device_id_type=MESH,
        )

    def project(target, part, order, c, result, weights):
        here = pl.ds(c * half, half)
        for j in range(0, blocks, 4):
            for source in order[j:j + 4]:
                copy = hand_over(target, part, source, c)

                @pl.when(core == c)
                def _():
                    piece = target.at[source, here, :]
                    pltpu.make_async_copy(piece, piece, r3.at[part, source]).wait()
                    copy.start()

                @pl.when(core != c)
                def _():
                    copy.wait_recv()

            flat = jnp.concatenate([target[source, here, :] for source in order[j:j + 4]], axis=0)
            for n, weight in enumerate(weights):
                made = mm(flat, weight[...])
                if n == 0:
                    made = made * 0.125
                for e, source in enumerate(order[j:j + 4]):
                    result[source, n, here, :] = made[e * half:(e + 1) * half].astype(bf16)

    fifth = []

    def attention(qkv, ret, many, owner_core, step, lanes, slot, part):
        def one_block(k, carry):
            block = ag_peer(-k)
            near_blocks = [nb_ref[j, block] for j in range(near)]
            for h in range(many):
                columns = slice(h * 128, (h + 1) * 128)
                query = two_heads(qkv[block, 0][:, columns])
                keys = jnp.concatenate([qkv[b, 1][:, columns] for b in near_blocks], axis=0)
                values = jnp.concatenate([qkv[b, 2][:, columns] for b in near_blocks], axis=0)
                scores = mm_nt(query, keys)
                weights = jnp.exp(scores - jnp.max(scores, axis=-1, keepdims=True))
                totals = jnp.sum(weights, axis=-1, keepdims=True)
                summed = mm(weights.astype(bf16), values)
                ret[k, :, columns] = join_heads(summed / totals).astype(bf16)
            return carry

        for k0 in (4, 6, 2, 0):
            lax.fori_loop(k0, k0 + 2, one_block, 0, unroll=2)
            for k in range(k0, k0 + 2):
                copy = pltpu.make_async_remote_copy(
                    src_ref=ret.at[k], dst_ref=am.at[step, :, lanes], send_sem=s5.at[part, k],
                    recv_sem=r5.at[step, slot],
                    device_id={"tm": tm - core + owner_core, "agent": ag_peer(-k)}, device_id_type=MESH,
                )
                if k:
                    copy.start()
                    fifth.append((None, copy))
                else:
                    stays = owner_core == core
                    own = pltpu.make_async_copy(ret.at[k], am.at[step, :, lanes], r5.at[step, slot])
                    pl.when(stays)(own.start)
                    pl.when(jnp.logical_not(stays))(copy.start)
                    fifth.append((stays, copy))

    def tail(where):
        for w in where:
            width = 256 if w < 4 else 128
            for slot in range(512 // width):
                target = am.at[w, :, pl.ds(slot * width, width)]
                pltpu.make_async_copy(target, target, r5.at[w, slot]).wait()
        both = jnp.concatenate([am[w] for w in where], axis=0)
        base = jnp.concatenate([aft_b[w] for w in where], axis=0).astype(f32)
        after_agent = (base + mm(both, woa[...])).astype(bf16).astype(f32)
        inner = jax.nn.gelu(mm(normed(after_agent), win[...]), approximate=True).astype(bf16)
        final = (after_agent + mm(inner, wmo[...])).astype(bf16)
        for n, w in enumerate(where):
            outs[w] = final[n * agents:(n + 1) * agents]

    for load in loads[6:12]:
        load.wait()
    of_full = (all_full, 0, full_order)
    of_part = (all_part, 1, part_order)
    project(*of_full, 0, qkv_full, (wqa, wka, wva))
    project(*of_part, 0, qkv_part, (wqb, wkb, wvb))
    project(*of_full, 1, qkv_full, (wqa, wka, wva))
    attention(qkv_full, ret_full, 2, full_core, full_step, full_lanes, core, 0)
    project(*of_part, 1, qkv_part, (wqb, wkb, wvb))
    attention(qkv_part, ret_part, 1, part_core, part_step, part_lanes, side * 2 + core, 1)
    for load in loads[12:]:
        load.wait()
    for w in range(0, steps, 2):
        tail([w, w + 1])

    for copy in unsent:
        copy.wait_send()
    for source in range(blocks):
        for part, target in ((0, all_full), (1, all_part)):
            hand_over(target, part, source, core).wait_send()
    for stays, copy in maybe + fifth:
        if stays is None:
            copy.wait_send()
        else:
            pl.when(jnp.logical_not(stays))(copy.wait_send)


def local(
    groups, blocks,
    states, neighbours, w_query_t, w_key_t, w_value_t, w_out_t, w_query_a, w_key_a, w_value_a, w_out_a, w_in, w_mlp_out,
):
    steps, agents, width = states.shape
    hidden = w_in.shape[1]
    rows = steps * (agents // groups)
    total = groups * steps
    square = (width, width)
    anywhere = pl.BlockSpec(memory_space=pl.ANY)
    dma = pltpu.SemaphoreType.DMA
    pieces = pltpu.VMEM((groups, rows, width), bf16)
    by_pair = pltpu.VMEM((width // 128, groups * rows, 128), f32)
    return pl.pallas_call(
        functools.partial(kernel, groups, blocks, steps, agents, neighbours.shape[1]),
        out_shape=pltpu.VMEM(states.shape, bf16),
        in_specs=[anywhere] * 12,
        out_specs=pl.BlockSpec(memory_space=pltpu.VMEM),
        scratch_shapes=[
            pltpu.SMEM(neighbours.shape[::-1], jnp.int32),
            pltpu.VMEM(states.shape, bf16),
            pltpu.VMEM(states.shape, f32),
            *[pltpu.VMEM(square, bf16)] * 4,
            *[pltpu.VMEM((width, 256), bf16)] * 3,
            *[pltpu.VMEM((width, 128), bf16)] * 3,
            pltpu.VMEM(square, bf16),
            pltpu.VMEM((width, hidden), bf16),
            pltpu.VMEM((hidden, width), bf16),
            pieces, pieces, by_pair, by_pair, by_pair,
            pltpu.VMEM((2 * total, total), f32),
            by_pair, pieces, pieces,
            pltpu.VMEM(states.shape, f32),
            pltpu.VMEM(states.shape, bf16),
            pltpu.VMEM(states.shape, bf16),
            pltpu.VMEM((blocks, agents, width), bf16),
            pltpu.VMEM((blocks, agents, width), bf16),
            pltpu.VMEM((blocks, 3, agents, 256), bf16),
            pltpu.VMEM((blocks, 3, agents, 128), bf16),
            pltpu.VMEM((blocks, agents, 256), bf16),
            pltpu.VMEM((blocks, agents, 128), bf16),
            pltpu.VMEM(states.shape, bf16),
            dma((15,)),
            dma((groups,)), dma((groups,)), dma((groups,)), dma((groups,)),
            dma((2, 4, 2)), dma((2, blocks)),
            dma((2, blocks)), dma((2, blocks)),
            dma((2, blocks)), dma((steps, 4)),
        ],
        compiler_params=pltpu.CompilerParams(
            collective_id=0, has_side_effects=True, vmem_limit_bytes=60 * 1024 * 1024
        ),
    )(states, neighbours.T, w_query_t, w_key_t, w_value_t, w_out_t, w_query_a, w_key_a, w_value_a, w_out_a, w_in, w_mlp_out)


def solution(mesh):
    placed = (P("tm", "agent", None), P(), P(), P(), P(), P(), P(), P(), P(), P(), P(), P())
    return jax.shard_map(
        functools.partial(local, mesh.shape["tm"], mesh.shape["agent"]),
        mesh=mesh, in_specs=placed, out_specs=P("tm", "agent", None), check_vma=False,
    )
```
